32 devices in a mesh: ens: 16 (over z, y, x), slab: 2 (over core).
Axes of the slice: x: 2, y: 2, z: 4, core: 2. Of those that a mesh axis runs over, the one named last changes fastest.
Arguments:
- ensemble: float32 [16, 3, 128, 768], P('ens', None, 'slab'), may hold values from -6 to 6
- perturbation: float32 [16, 3, 128, 768], P('ens', None, 'slab'), may hold values from -6 to 6
- ancestors: int32 [16], P('ens'), may hold values from 0 to 15
- bathymetry: int32 [128, 768], replicated, may hold values from 50 to 200
Outputs:
- analysis: float32 [16, 3, 128, 768], P('ens', None, 'slab')
The draws below stay inside these ranges and needn't reach their ends.
Inputs may be any that keep to these rules, and one draw needn't show every extreme that they name: `ancestors`: each entry names the old particle that a new particle copies.
All inputs are finite; a program needn't handle non-finite values.
Results may differ from the reference program's by a relative error of at most 0.00002.
Values sent between devices are 32-bit elements; how exact they have to be, the bound alone decides.
A program may use at most 128 MiB of HBM per device.

```python
import jax
import jax.numpy as jnp
from jax import lax

NX = 768
STEPS = 3
PARTICLES = 16
NY = 128


def place_ends(drawn, key, smallest, top_value):
    dims = drawn.shape
    spot = [jax.random.randint(jax.random.fold_in(key, axis), (), 0, dims[axis]) for axis in range(len(dims))]
    drawn = drawn.at[tuple(spot)].set(smallest)
    longest = dims.index(max(dims))
    spot[longest] = (spot[longest] + 1) % dims[longest]
    return drawn.at[tuple(spot)].set(top_value)


def shard_levels(rng, dims, shards, low, top_value):
    def one(axis_at, shards_of):
        steps = jax.random.uniform(jax.random.fold_in(jax.random.fold_in(rng, 6), axis_at), (shards_of,), jnp.float32, low / len(shards), top_value / len(shards))
        return jnp.repeat(jnp.exp(steps), dims[axis_at] // shards_of).reshape((-1,) + (1,) * (len(dims) - axis_at - 1))

    loudness = one(*shards[0])
    for cut in shards[1:]:
        loudness = loudness * one(*cut)
    return loudness


def noise(own_key, extent, scale, limit, split=(), dtype=jnp.bfloat16):
    array = jax.random.normal(own_key, extent, jnp.float32) * scale
    if len(split) > 0:
        array = shard_levels(own_key, extent, split, -0.22, 0.18) * array
    return jnp.clip(array, min=-limit, max=limit).astype(dtype)


def setup_inputs(seed: int = 0) -> dict:
    seeds = jax.random.split(jax.random.key(seed), 5)
    return {
        "ensemble": noise(seeds[0], (PARTICLES, 3, NY, NX), 1.0, 6.0, ((0, 16), (2, 2)), jnp.float32),
        "perturbation": noise(seeds[1], (PARTICLES, 3, NY, NX), 1.0, 6.0, ((0, 16), (2, 2)), jnp.float32),
        "ancestors": place_ends(jax.random.randint(seeds[2], (PARTICLES,), 0, PARTICLES), jax.random.fold_in(seeds[2], 1), 0, PARTICLES - 1).astype(jnp.int32),
        "bathymetry": place_ends(jax.random.randint(seeds[3], (NY, NX), 50, 201), jax.random.fold_in(seeds[3], 1), 50, 200).astype(jnp.int32),
    }


RATIO = 0.3
TURNING = 0.03
JITTER = 0.5


def eastward_difference(field):
    return (jnp.roll(field, -1, -1) - jnp.roll(field, 1, -1)) * 0.5


def northward_difference(field):
    padded = jnp.pad(field, ((1, 1), (0, 0)))
    return (padded[2:] - padded[:-2]) * 0.5


def integrate_forward(ensemble_member, ocean_floor):
    height, east_vel, north_vel = ensemble_member[0], ensemble_member[1], ensemble_member[2]
    for substep in range(STEPS):
        flux_east = ocean_floor * east_vel
        flux_north = ocean_floor * north_vel
        height = height - RATIO * (eastward_difference(flux_east) + northward_difference(flux_north))
        east_next = east_vel - RATIO * eastward_difference(height) + TURNING * north_vel
        north_next = north_vel - RATIO * northward_difference(height) - TURNING * east_vel
        east_vel, north_vel = east_next, north_next
    return jnp.stack([height, east_vel, north_vel])


def smoothed_noise(ensemble_member):
    padded = jnp.pad(ensemble_member, ((0, 0), (1, 1), (0, 0)))
    return (4.0 * ensemble_member + padded[:, 2:] + padded[:, :-2] + jnp.roll(ensemble_member, 1, -1) + jnp.roll(ensemble_member, -1, -1)) * 0.125


def reference(ensemble, perturbation, ancestors, bathymetry):
    ocean_floor = bathymetry.astype(jnp.float32) * 0.01
    predicted_state = lax.map(lambda ensemble_member: integrate_forward(ensemble_member, ocean_floor), ensemble)
    selected_parents = jnp.take(predicted_state, ancestors.astype(jnp.int32), axis=0)
    return selected_parents + JITTER * lax.map(smoothed_noise, perturbation)
```

```python
import functools

import jax
import jax.numpy as jnp
from jax import lax
from jax.experimental import pallas as pl
from jax.experimental.pallas import tpu as pltpu
from jax.sharding import PartitionSpec as P

STEPS = 3
MESH = pl.DeviceIdType.MESH
STRIP = 8
LANES = 128


RATIO = 0.3
TURNING = 0.03
JITTER = 0.5


def padded(cells, sides, width):
    for axis, dim in sides:
        count = lax.axis_size(axis)
        ends = count - 1
        head = lax.slice_in_dim(cells, 0, width, axis=dim)
        tail = lax.slice_in_dim(cells, cells.shape[dim] - width, cells.shape[dim], axis=dim)
        cells = jnp.concatenate(
            [
                lax.ppermute(tail, axis, [(i, (i + 1) % count) for i in range(ends)]),
                cells,
                lax.ppermute(head, axis, [((i + 1) % count, i) for i in range(ends)]),
            ],
            axis=dim,
        )
    return cells


def eastward_difference(field):
    return (jnp.roll(field, -1, -1) - jnp.roll(field, 1, -1)) * 0.5


def step_rows(height, east_vel, north_vel, ocean_floor, inside):
    flux_east = ocean_floor * east_vel
    flux_north = ocean_floor * north_vel
    height_next = height[1:-1] - RATIO * (
        eastward_difference(flux_east[1:-1]) + (flux_north[2:] - flux_north[:-2]) * 0.5
    )
    height_next = jnp.where(inside[1:-1], height_next, 0.0)
    east_next = (
        east_vel[2:-2] - RATIO * eastward_difference(height_next[1:-1]) + TURNING * north_vel[2:-2]
    )
    north_next = (
        north_vel[2:-2]
        - RATIO * (height_next[2:] - height_next[:-2]) * 0.5
        - TURNING * east_vel[2:-2]
    )
    kept = inside[2:-2]
    return (height_next[1:-1], jnp.where(kept, east_next, 0.0), jnp.where(kept, north_next, 0.0))


def edge_rows(members, depth):
    return jnp.stack(
        [jnp.concatenate([member[:depth], member[-depth:]], axis=0) for member in members]
    )


def attach_rims(members, rims, depth):
    return [
        jnp.concatenate([rims[k, :depth], members[k], rims[k, 3 * depth :]], axis=0)
        for k in range(len(members))
    ]


def pick_rows(portion, lineage):
    return jnp.take(portion, lineage, axis=0, mode="clip")


def shards(ensemble, perturbation, ancestors, bathymetry):
    row_count = ensemble.shape[2]
    col_count = ensemble.shape[3]
    total_rows = bathymetry.shape[0]
    first_row = lax.axis_index("slab") * row_count
    widest = 2 * STEPS
    seabed_all = jnp.pad(bathymetry.astype(jnp.float32) * 0.01, ((widest, widest), (0, 0)))
    members = [ensemble[0, 0], ensemble[0, 1], ensemble[0, 2]]
    ocean_floor = lax.dynamic_slice_in_dim(seabed_all, first_row + widest - 2, row_count + 2 * 2, 0)
    global_row = first_row - 2 + jnp.arange(row_count + 2 * 2, dtype=jnp.int32)
    inside = ((global_row >= 0) & (global_row < total_rows))[:, None]
    ocean_floor, inside = (ocean_floor, inside)
    for substep in range(STEPS):
        rims = padded(edge_rows(members, 2), (("slab", 1),), 2)
        widened = attach_rims(members, rims, 2)
        members = list(step_rows(widened[0], widened[1], widened[2], ocean_floor, inside))
    noise = [perturbation[0, 0], perturbation[0, 1], perturbation[0, 2]]
    noise_rims = padded(edge_rows(noise, 1), (("slab", 1),), 1)
    bordered = attach_rims(noise, noise_rims, 1)
    smoothed = jnp.stack(
        [
            (
                4.0 * cell[1:-1]
                + cell[2:]
                + cell[:-2]
                + jnp.roll(cell[1:-1], 1, -1)
                + jnp.roll(cell[1:-1], -1, -1)
            )
            * 0.125
            for cell in bordered
        ]
    )
    lineage = lax.all_gather(ancestors, "ens", axis=0, tiled=True)
    flattened = jnp.stack(members).reshape(1, 3, row_count * col_count)
    pieces = lax.all_to_all(flattened, "ens", split_axis=2, concat_axis=0, tiled=True)
    picked = pick_rows(pieces, lineage)
    returned = lax.all_to_all(picked, "ens", split_axis=0, concat_axis=2, tiled=True)
    selected_parents = returned.reshape(1, 3, row_count, col_count)
    return selected_parents + JITTER * smoothed[None]


def whole_wait(ref, sem):
    pltpu.make_async_copy(ref, ref, sem).wait()


def cycle_kernel(
    n, rows, cols, across,
    ens_ref, pert_ref, anc_ref, bath_ref, out_ref,
    state, noise, sb, pieces0, pieces1, pieces2, picked, res, lin_v, lin_s,
    halo_send, halo_recv, lin_send, lin_recv, lin_local,
    a_send, a_recv, b_send, b_recv,
):
    me = lax.axis_index("ens")
    s = lax.axis_index("slab")
    width = cols // across
    pieces = (pieces0, pieces1, pieces2)
    top = STRIP
    bottom = STRIP + rows
    barrier = pltpu.get_barrier_semaphore()

    def peer(t):
        offset = n // 2 + (1 - 2 * (t % 2)) * ((t + 1) // 2)
        return lax.rem(me + offset, n)

    def each_peer(body):
        def run(t, carry):
            body(t, peer(t))
            return carry

        lax.fori_loop(0, n - 1, run, 0)

    def greet(t, to):
        pl.semaphore_signal(barrier, inc=1, device_id={"ens": to}, device_id_type=MESH)

    each_peer(greet)
    pl.semaphore_signal(barrier, inc=1, device_id={"slab": 1 - s}, device_id_type=MESH)

    lin_v[me] = jnp.full((1, LANES), anc_ref[0], jnp.int32)
    wall = pl.multiple_of(s * (rows + STRIP), STRIP)
    open_side = pl.multiple_of((1 - s) * (rows + STRIP), STRIP)
    zeros = jnp.zeros((STRIP, cols), jnp.float32)
    for f in range(3):
        state[f, pl.ds(wall, STRIP)] = zeros
        noise[f, pl.ds(wall, STRIP)] = zeros
        for r in range(0, rows, STRIP):
            state[f, top + r : top + r + STRIP] = ens_ref[f, r : r + STRIP]
            noise[f, top + r : top + r + STRIP] = pert_ref[f, r : r + STRIP]
    sb[pl.ds(wall, STRIP)] = zeros
    beyond = pl.multiple_of(rows - STRIP * s, STRIP)
    sb[pl.ds(open_side, STRIP)] = bath_ref[pl.ds(beyond, STRIP)].astype(jnp.float32) * 0.01
    first = pl.multiple_of(s * rows, STRIP)
    for r in range(0, rows, STRIP):
        sb[top + r : top + r + STRIP] = (
            bath_ref[pl.ds(pl.multiple_of(first + r, STRIP), STRIP)].astype(jnp.float32) * 0.01
        )

    pl.semaphore_wait(barrier, n)

    edge = pl.multiple_of((1 - s) * (rows - STRIP), STRIP)
    halos = []
    for i, (src, dst) in enumerate(((ens_ref, state), (pert_ref, noise))):
        copy = pltpu.make_async_remote_copy(
            src_ref=src.at[:, pl.ds(edge, STRIP)],
            dst_ref=dst.at[:, pl.ds(wall, STRIP)],
            send_sem=halo_send.at[i],
            recv_sem=halo_recv.at[i],
            device_id={"slab": 1 - s},
            device_id_type=MESH,
        )
        copy.start()
        halos.append(copy)

    def tell(t, to):
        pltpu.make_async_remote_copy(
            src_ref=lin_v.at[me],
            dst_ref=lin_v.at[me],
            send_sem=lin_send,
            recv_sem=lin_recv,
            device_id={"ens": to},
            device_id_type=MESH,
        ).start()

    each_peer(tell)
    halos[0].wait()

    def shifted(f, r, by):
        source = sb if f is None else state.at[f]
        if 0 <= r + by <= rows + STRIP:
            return source[r + by : r + by + STRIP]
        return pltpu.roll(source[r : r + STRIP], -by % STRIP, 0)

    def east(x):
        return (pltpu.roll(x, cols - 1, 1) - pltpu.roll(x, 1, 1)) * 0.5

    def heights(r):
        here = slice(r, r + STRIP)
        northward = shifted(None, r, 1) * shifted(2, r, 1) - shifted(None, r, -1) * shifted(2, r, -1)
        new = state[0, here] - RATIO * (east(sb[here] * state[1, here]) + northward * 0.5)
        if r == 0:
            new = jnp.where(s == 1, new, 0.0)
        if r == bottom:
            new = jnp.where(s == 0, new, 0.0)
        state[0, here] = new

    def velocities(r):
        here = slice(r, r + STRIP)
        u = state[1, here]
        v = state[2, here]
        state[1, here] = u - RATIO * east(state[0, here]) + TURNING * v
        northward = (shifted(0, r, 1) - shifted(0, r, -1)) * 0.5
        state[2, here] = v - RATIO * northward - TURNING * u

    def spot(ref, f, index, base):
        r = pl.multiple_of(base + (index // across) * STRIP, STRIP)
        c = pl.multiple_of((index % across) * width, LANES)
        return ref.at[f, pl.ds(r, STRIP), pl.ds(c, width)]

    def scatter(f):
        def send(t, to):
            pltpu.make_async_remote_copy(
                src_ref=spot(state, f, to, top),
                dst_ref=pieces[f].at[me],
                send_sem=a_send.at[f],
                recv_sem=a_recv.at[f],
                device_id={"ens": to},
                device_id_type=MESH,
            ).start()

        each_peer(send)
        pltpu.make_async_copy(spot(state, f, me, top), pieces[f].at[me], a_recv.at[f]).start()

    for step in range(STEPS):
        last = step == STEPS - 1
        for r in range(0, bottom + STRIP, STRIP):
            heights(r)
        if last:
            scatter(0)
        for r in range(top if last else 0, bottom if last else bottom + STRIP, STRIP):
            velocities(r)
    scatter(1)
    scatter(2)

    halos[1].wait()
    for f in range(3):
        for r in range(top, bottom, STRIP):
            p = noise[f, r : r + STRIP]
            around = noise[f, r + 1 : r + 1 + STRIP] + noise[f, r - 1 : r - 1 + STRIP]
            total = 4.0 * p + around + pltpu.roll(p, 1, 1) + pltpu.roll(p, cols - 1, 1)
            out_ref[f, r - top : r - top + STRIP] = total * 0.125 * JITTER

    whole_wait(lin_v.at[pl.ds(0, n - 1)], lin_recv)
    fetch = pltpu.make_async_copy(lin_v, lin_s, lin_local)
    fetch.start()
    fetch.wait()

    for f in range(3):
        whole_wait(pieces[f], a_recv.at[f])

        def reply(t, to):
            picked[f, t] = pieces[f][lin_s[to, 0, 0]]
            pltpu.make_async_remote_copy(
                src_ref=picked.at[f, t],
                dst_ref=spot(res, f, me, 0),
                send_sem=b_send.at[f],
                recv_sem=b_recv.at[f],
                device_id={"ens": to},
                device_id_type=MESH,
            ).start()

        each_peer(reply)
        picked[f, n - 1] = pieces[f][lin_s[me, 0, 0]]
        pltpu.make_async_copy(picked.at[f, n - 1], spot(res, f, me, 0), b_recv.at[f]).start()

    for f in range(3):
        whole_wait(res.at[f], b_recv.at[f])
        for r in range(0, rows, STRIP):
            out_ref[f, r : r + STRIP] = res[f, r : r + STRIP] + out_ref[f, r : r + STRIP]
    whole_wait(lin_v.at[pl.ds(0, n - 1)], lin_send)
    for f in range(3):
        whole_wait(pieces[f].at[pl.ds(0, n - 1)], a_send.at[f])
        whole_wait(picked.at[f, pl.ds(0, n - 1)], b_send.at[f])


def cycle(n, ensemble, perturbation, ancestors, bathymetry):
    rows, cols = ensemble.shape[2:]
    across = n * STRIP // rows
    tall = rows + 2 * STRIP
    f32 = jnp.float32
    vmem = pl.BlockSpec(memory_space=pltpu.VMEM)
    dma = pltpu.SemaphoreType.DMA
    result = pl.pallas_call(
        functools.partial(cycle_kernel, n, rows, cols, across),
        out_shape=jax.ShapeDtypeStruct((3, rows, cols), f32),
        in_specs=[vmem, vmem, pl.BlockSpec(memory_space=pltpu.SMEM), vmem],
        out_specs=vmem,
        scratch_shapes=[
            pltpu.VMEM((3, tall, cols), f32),
            pltpu.VMEM((3, tall, cols), f32),
            pltpu.VMEM((tall, cols), f32),
            pltpu.VMEM((n, STRIP, cols // across), f32),
            pltpu.VMEM((n, STRIP, cols // across), f32),
            pltpu.VMEM((n, STRIP, cols // across), f32),
            pltpu.VMEM((3, n, STRIP, cols // across), f32),
            pltpu.VMEM((3, rows, cols), f32),
            pltpu.VMEM((n, 1, LANES), jnp.int32),
            pltpu.SMEM((n, 1, LANES), jnp.int32),
            dma((2,)), dma((2,)), dma(()), dma(()), dma(()),
            dma((3,)), dma((3,)), dma((3,)), dma((3,)),
        ],
        compiler_params=pltpu.CompilerParams(collective_id=0, has_side_effects=True),
        name="cycle",
    )(ensemble[0], perturbation[0], ancestors, bathymetry)
    return result[None]


def fits(mesh, ensemble):
    n, slabs = mesh.shape["ens"], mesh.shape["slab"]
    rows, cols = ensemble.shape[2] // slabs, ensemble.shape[3]
    strips = rows // STRIP
    if slabs != 2 or ensemble.shape[0] != n or rows % STRIP or n % strips:
        return False
    across = n // strips
    return cols % (across * LANES) == 0


def solution(mesh):
    in_specs = (P("ens", None, "slab", None), P("ens", None, "slab", None), P("ens"), P())
    out_specs = P("ens", None, "slab", None)

    def run(ensemble, perturbation, ancestors, bathymetry):
        body = functools.partial(cycle, mesh.shape["ens"]) if fits(mesh, ensemble) else shards
        mapped = jax.shard_map(body, mesh=mesh, in_specs=in_specs, out_specs=out_specs, check_vma=False)
        return mapped(ensemble, perturbation, ancestors, bathymetry)

    return run
```

```python
import functools

import jax
import jax.numpy as jnp
from jax import lax
from jax.experimental import pallas as pl
from jax.experimental.pallas import tpu as pltpu
from jax.sharding import PartitionSpec as P

STEPS = 3
MESH = pl.DeviceIdType.MESH
STRIP = 8
LANES = 128


RATIO = 0.3
TURNING = 0.03
JITTER = 0.5


def padded(cells, sides, width):
    for axis, dim in sides:
        count = lax.axis_size(axis)
        ends = count - 1
        head = lax.slice_in_dim(cells, 0, width, axis=dim)
        tail = lax.slice_in_dim(cells, cells.shape[dim] - width, cells.shape[dim], axis=dim)
        cells = jnp.concatenate(
            [
                lax.ppermute(tail, axis, [(i, (i + 1) % count) for i in range(ends)]),
                cells,
                lax.ppermute(head, axis, [((i + 1) % count, i) for i in range(ends)]),
            ],
            axis=dim,
        )
    return cells


def eastward_difference(field):
    return (jnp.roll(field, -1, -1) - jnp.roll(field, 1, -1)) * 0.5


def step_rows(height, east_vel, north_vel, ocean_floor, inside):
    flux_east = ocean_floor * east_vel
    flux_north = ocean_floor * north_vel
    height_next = height[1:-1] - RATIO * (
        eastward_difference(flux_east[1:-1]) + (flux_north[2:] - flux_north[:-2]) * 0.5
    )
    height_next = jnp.where(inside[1:-1], height_next, 0.0)
    east_next = (
        east_vel[2:-2] - RATIO * eastward_difference(height_next[1:-1]) + TURNING * north_vel[2:-2]
    )
    north_next = (
        north_vel[2:-2]
        - RATIO * (height_next[2:] - height_next[:-2]) * 0.5
        - TURNING * east_vel[2:-2]
    )
    kept = inside[2:-2]
    return (height_next[1:-1], jnp.where(kept, east_next, 0.0), jnp.where(kept, north_next, 0.0))


def edge_rows(members, depth):
    return jnp.stack(
        [jnp.concatenate([member[:depth], member[-depth:]], axis=0) for member in members]
    )


def attach_rims(members, rims, depth):
    return [
        jnp.concatenate([rims[k, :depth], members[k], rims[k, 3 * depth :]], axis=0)
        for k in range(len(members))
    ]


def pick_rows(portion, lineage):
    return jnp.take(portion, lineage, axis=0, mode="clip")


def shards(ensemble, perturbation, ancestors, bathymetry):
    row_count = ensemble.shape[2]
    col_count = ensemble.shape[3]
    total_rows = bathymetry.shape[0]
    first_row = lax.axis_index("slab") * row_count
    widest = 2 * STEPS
    seabed_all = jnp.pad(bathymetry.astype(jnp.float32) * 0.01, ((widest, widest), (0, 0)))
    members = [ensemble[0, 0], ensemble[0, 1], ensemble[0, 2]]
    ocean_floor = lax.dynamic_slice_in_dim(seabed_all, first_row + widest - 2, row_count + 2 * 2, 0)
    global_row = first_row - 2 + jnp.arange(row_count + 2 * 2, dtype=jnp.int32)
    inside = ((global_row >= 0) & (global_row < total_rows))[:, None]
    ocean_floor, inside = (ocean_floor, inside)
    for substep in range(STEPS):
        rims = padded(edge_rows(members, 2), (("slab", 1),), 2)
        widened = attach_rims(members, rims, 2)
        members = list(step_rows(widened[0], widened[1], widened[2], ocean_floor, inside))
    noise = [perturbation[0, 0], perturbation[0, 1], perturbation[0, 2]]
    noise_rims = padded(edge_rows(noise, 1), (("slab", 1),), 1)
    bordered = attach_rims(noise, noise_rims, 1)
    smoothed = jnp.stack(
        [
            (
                4.0 * cell[1:-1]
                + cell[2:]
                + cell[:-2]
                + jnp.roll(cell[1:-1], 1, -1)
                + jnp.roll(cell[1:-1], -1, -1)
            )
            * 0.125
            for cell in bordered
        ]
    )
    lineage = lax.all_gather(ancestors, "ens", axis=0, tiled=True)
    flattened = jnp.stack(members).reshape(1, 3, row_count * col_count)
    pieces = lax.all_to_all(flattened, "ens", split_axis=2, concat_axis=0, tiled=True)
    picked = pick_rows(pieces, lineage)
    returned = lax.all_to_all(picked, "ens", split_axis=0, concat_axis=2, tiled=True)
    selected_parents = returned.reshape(1, 3, row_count, col_count)
    return selected_parents + JITTER * smoothed[None]


def whole_wait(ref, sem):
    pltpu.make_async_copy(ref, ref, sem).wait()


def cycle_kernel(
    n, rows, cols, across,
    ens_ref, pert_ref, anc_ref, bath_ref, out_ref,
    state, noise, sb, seam, seam_sb, pieces0, pieces1, pieces2, picked, res, lin_v, lin_s,
    halo_send, halo_recv, lin_send, lin_recv, lin_local,
    a_send, a_recv, b_send, b_recv,
):
    me = lax.axis_index("ens")
    s = lax.axis_index("slab")
    width = cols // across
    pieces = (pieces0, pieces1, pieces2)
    top = STRIP
    bottom = STRIP + rows
    barrier = pltpu.get_barrier_semaphore()

    def peer(t):
        offset = n // 2 + (1 - 2 * (t % 2)) * ((t + 1) // 2)
        return lax.rem(me + offset, n)

    def each_peer(body):
        def run(t, carry):
            body(t, peer(t))
            return carry

        lax.fori_loop(0, n - 1, run, 0)

    def greet(t, to):
        pl.semaphore_signal(barrier, inc=1, device_id={"ens": to}, device_id_type=MESH)

    each_peer(greet)
    pl.semaphore_signal(barrier, inc=1, device_id={"slab": 1 - s}, device_id_type=MESH)

    lin_v[me] = jnp.full((1, LANES), anc_ref[0], jnp.int32)
    zeros = jnp.zeros((STRIP, cols), jnp.float32)
    first = pl.multiple_of(s * rows, STRIP)
    for r in (0, bottom):
        sb[r : r + STRIP] = zeros
        for f in range(3):
            state[f, r : r + STRIP] = zeros
    for r in range(0, rows, STRIP):
        depth = bath_ref[pl.ds(pl.multiple_of(first + r, STRIP), STRIP)]
        sb[top + r : top + r + STRIP] = depth.astype(jnp.float32) * 0.01
        for f in range(3):
            state[f, top + r : top + r + STRIP] = ens_ref[f, r : r + STRIP]
    inner = pl.multiple_of((1 - s) * (rows - 2 * STRIP), STRIP)
    for r in range(0, 3 * STRIP, STRIP):
        depth = bath_ref[pl.ds(pl.multiple_of(rows - 2 * STRIP + s * STRIP + r, STRIP), STRIP)]
        seam_sb[r : r + STRIP] = depth.astype(jnp.float32) * 0.01
    for f in range(3):
        for r in range(0, 2 * STRIP, STRIP):
            seam[f, pl.ds(pl.multiple_of(s * STRIP + r, STRIP), STRIP)] = ens_ref[
                f, pl.ds(pl.multiple_of(inner + r, STRIP), STRIP)
            ]

    def east(x):
        return (pltpu.roll(x, cols - 1, 1) - pltpu.roll(x, 1, 1)) * 0.5

    def shifted(ref, r, by):
        if 0 <= r + by <= ref.shape[0] - STRIP:
            return ref[r + by : r + by + STRIP]
        return pltpu.roll(ref[r : r + STRIP], -by % STRIP, 0)

    def heights(cells, floor, r):
        here = slice(r, r + STRIP)
        v = cells.at[2]
        northward = shifted(floor, r, 1) * shifted(v, r, 1) - shifted(floor, r, -1) * shifted(v, r, -1)
        eastward = east(floor[here] * cells[1, here])
        cells[0, here] = cells[0, here] - RATIO * (eastward + northward * 0.5)

    def velocities(cells, r):
        here = slice(r, r + STRIP)
        u = cells[1, here]
        v = cells[2, here]
        h = cells.at[0]
        cells[1, here] = u - RATIO * east(h[here]) + TURNING * v
        northward = (shifted(h, r, 1) - shifted(h, r, -1)) * 0.5
        cells[2, here] = v - RATIO * northward - TURNING * u

    for step in range(STEPS):
        for r in range(top, bottom, STRIP):
            heights(state, sb, r)
        for r in range(top, bottom, STRIP):
            velocities(state, r)

    pl.semaphore_wait(barrier, n)

    edge = pl.multiple_of((1 - s) * (rows - STRIP), STRIP)
    halos = []
    for i, (src, dst, at) in enumerate(
        ((ens_ref, seam, s * 2 * STRIP), (pert_ref, noise, s * (rows + STRIP)))
    ):
        copy = pltpu.make_async_remote_copy(
            src_ref=src.at[:, pl.ds(edge, STRIP)],
            dst_ref=dst.at[:, pl.ds(pl.multiple_of(at, STRIP), STRIP)],
            send_sem=halo_send.at[i],
            recv_sem=halo_recv.at[i],
            device_id={"slab": 1 - s},
            device_id_type=MESH,
        )
        copy.start()
        halos.append(copy)

    def spot(ref, f, index, base):
        r = pl.multiple_of(base + (index // across) * STRIP, STRIP)
        c = pl.multiple_of((index % across) * width, LANES)
        return ref.at[f, pl.ds(r, STRIP), pl.ds(c, width)]

    def deliver(f, to):
        pltpu.make_async_remote_copy(
            src_ref=spot(state, f, to, top),
            dst_ref=pieces[f].at[me],
            send_sem=a_send.at[f],
            recv_sem=a_recv.at[f],
            device_id={"ens": to},
            device_id_type=MESH,
        ).start()

    def keep(f):
        pltpu.make_async_copy(spot(state, f, me, top), pieces[f].at[me], a_recv.at[f]).start()

    def at_seam(to):
        return to // across == (1 - s) * (rows // STRIP - 1)

    def early(t, to):
        @pl.when(jnp.logical_not(at_seam(to)))
        def _():
            deliver(0, to)

    each_peer(early)

    def tell(t, to):
        pltpu.make_async_remote_copy(
            src_ref=lin_v.at[me],
            dst_ref=lin_v.at[me],
            send_sem=lin_send,
            recv_sem=lin_recv,
            device_id={"ens": to},
            device_id_type=MESH,
        ).start()

    each_peer(tell)
    halos[0].wait()
    for step in range(STEPS):
        last = step == STEPS - 1
        for r in range(0, 3 * STRIP, STRIP):
            heights(seam, seam_sb, r)
        for r in range(STRIP, 2 * STRIP, STRIP) if last else range(0, 3 * STRIP, STRIP):
            velocities(seam, r)
    for f in range(3):
        state[f, pl.ds(pl.multiple_of(top + edge, STRIP), STRIP)] = seam[f, STRIP : 2 * STRIP]

    def late(t, to):
        @pl.when(at_seam(to))
        def _():
            deliver(0, to)

    each_peer(late)
    keep(0)
    for f in (1, 2):
        each_peer(lambda t, to, f=f: deliver(f, to))
        keep(f)

    wall = pl.multiple_of(s * (rows + STRIP), STRIP)
    for f in range(3):
        noise[f, pl.ds(wall, STRIP)] = zeros
        for r in range(0, rows, STRIP):
            noise[f, top + r : top + r + STRIP] = pert_ref[f, r : r + STRIP]
    halos[1].wait()
    for f in range(3):
        for r in range(top, bottom, STRIP):
            p = noise[f, r : r + STRIP]
            around = noise[f, r + 1 : r + 1 + STRIP] + noise[f, r - 1 : r - 1 + STRIP]
            total = 4.0 * p + around + pltpu.roll(p, 1, 1) + pltpu.roll(p, cols - 1, 1)
            out_ref[f, r - top : r - top + STRIP] = total * 0.125 * JITTER

    whole_wait(lin_v.at[pl.ds(0, n - 1)], lin_recv)
    fetch = pltpu.make_async_copy(lin_v, lin_s, lin_local)
    fetch.start()
    fetch.wait()

    for f in range(3):
        whole_wait(pieces[f], a_recv.at[f])

        def reply(t, to):
            picked[f, t] = pieces[f][lin_s[to, 0, 0]]
            pltpu.make_async_remote_copy(
                src_ref=picked.at[f, t],
                dst_ref=spot(res, f, me, 0),
                send_sem=b_send.at[f],
                recv_sem=b_recv.at[f],
                device_id={"ens": to},
                device_id_type=MESH,
            ).start()

        each_peer(reply)
        picked[f, n - 1] = pieces[f][lin_s[me, 0, 0]]
        pltpu.make_async_copy(picked.at[f, n - 1], spot(res, f, me, 0), b_recv.at[f]).start()

    for f in range(3):
        whole_wait(res.at[f], b_recv.at[f])
        for r in range(0, rows, STRIP):
            out_ref[f, r : r + STRIP] = res[f, r : r + STRIP] + out_ref[f, r : r + STRIP]
    whole_wait(lin_v.at[pl.ds(0, n - 1)], lin_send)
    for f in range(3):
        whole_wait(pieces[f].at[pl.ds(0, n - 1)], a_send.at[f])
        whole_wait(picked.at[f, pl.ds(0, n - 1)], b_send.at[f])


def cycle(n, ensemble, perturbation, ancestors, bathymetry):
    rows, cols = ensemble.shape[2:]
    across = n * STRIP // rows
    tall = rows + 2 * STRIP
    f32 = jnp.float32
    vmem = pl.BlockSpec(memory_space=pltpu.VMEM)
    dma = pltpu.SemaphoreType.DMA
    result = pl.pallas_call(
        functools.partial(cycle_kernel, n, rows, cols, across),
        out_shape=jax.ShapeDtypeStruct((3, rows, cols), f32),
        in_specs=[vmem, vmem, pl.BlockSpec(memory_space=pltpu.SMEM), vmem],
        out_specs=vmem,
        scratch_shapes=[
            pltpu.VMEM((3, tall, cols), f32),
            pltpu.VMEM((3, tall, cols), f32),
            pltpu.VMEM((tall, cols), f32),
            pltpu.VMEM((3, 3 * STRIP, cols), f32),
            pltpu.VMEM((3 * STRIP, cols), f32),
            pltpu.VMEM((n, STRIP, cols // across), f32),
            pltpu.VMEM((n, STRIP, cols // across), f32),
            pltpu.VMEM((n, STRIP, cols // across), f32),
            pltpu.VMEM((3, n, STRIP, cols // across), f32),
            pltpu.VMEM((3, rows, cols), f32),
            pltpu.VMEM((n, 1, LANES), jnp.int32),
            pltpu.SMEM((n, 1, LANES), jnp.int32),
            dma((2,)), dma((2,)), dma(()), dma(()), dma(()),
            dma((3,)), dma((3,)), dma((3,)), dma((3,)),
        ],
        compiler_params=pltpu.CompilerParams(collective_id=0, has_side_effects=True),
        name="cycle",
    )(ensemble[0], perturbation[0], ancestors, bathymetry)
    return result[None]


def fits(mesh, ensemble):
    n, slabs = mesh.shape["ens"], mesh.shape["slab"]
    rows, cols = ensemble.shape[2] // slabs, ensemble.shape[3]
    strips = rows // STRIP
    if slabs != 2 or ensemble.shape[0] != n or rows % STRIP or n % strips:
        return False
    across = n // strips
    return cols % (across * LANES) == 0


def solution(mesh):
    in_specs = (P("ens", None, "slab", None), P("ens", None, "slab", None), P("ens"), P())
    out_specs = P("ens", None, "slab", None)

    def run(ensemble, perturbation, ancestors, bathymetry):
        body = functools.partial(cycle, mesh.shape["ens"]) if fits(mesh, ensemble) else shards
        mapped = jax.shard_map(body, mesh=mesh, in_specs=in_specs, out_specs=out_specs, check_vma=False)
        return mapped(ensemble, perturbation, ancestors, bathymetry)

    return run
```

```python
import functools

import jax
import jax.numpy as jnp
from jax import lax
from jax.experimental import pallas as pl
from jax.experimental.pallas import tpu as pltpu
from jax.sharding import PartitionSpec as P

STEPS = 3
MESH = pl.DeviceIdType.MESH
STRIP = 8
LANES = 128


RATIO = 0.3
TURNING = 0.03
JITTER = 0.5


def padded(cells, sides, width):
    for axis, dim in sides:
        count = lax.axis_size(axis)
        ends = count - 1
        head = lax.slice_in_dim(cells, 0, width, axis=dim)
        tail = lax.slice_in_dim(cells, cells.shape[dim] - width, cells.shape[dim], axis=dim)
        cells = jnp.concatenate(
            [
                lax.ppermute(tail, axis, [(i, (i + 1) % count) for i in range(ends)]),
                cells,
                lax.ppermute(head, axis, [((i + 1) % count, i) for i in range(ends)]),
            ],
            axis=dim,
        )
    return cells


def eastward_difference(field):
    return (jnp.roll(field, -1, -1) - jnp.roll(field, 1, -1)) * 0.5


def step_rows(height, east_vel, north_vel, ocean_floor, inside):
    flux_east = ocean_floor * east_vel
    flux_north = ocean_floor * north_vel
    height_next = height[1:-1] - RATIO * (
        eastward_difference(flux_east[1:-1]) + (flux_north[2:] - flux_north[:-2]) * 0.5
    )
    height_next = jnp.where(inside[1:-1], height_next, 0.0)
    east_next = (
        east_vel[2:-2] - RATIO * eastward_difference(height_next[1:-1]) + TURNING * north_vel[2:-2]
    )
    north_next = (
        north_vel[2:-2]
        - RATIO * (height_next[2:] - height_next[:-2]) * 0.5
        - TURNING * east_vel[2:-2]
    )
    kept = inside[2:-2]
    return (height_next[1:-1], jnp.where(kept, east_next, 0.0), jnp.where(kept, north_next, 0.0))


def edge_rows(members, depth):
    return jnp.stack(
        [jnp.concatenate([member[:depth], member[-depth:]], axis=0) for member in members]
    )


def attach_rims(members, rims, depth):
    return [
        jnp.concatenate([rims[k, :depth], members[k], rims[k, 3 * depth :]], axis=0)
        for k in range(len(members))
    ]


def pick_rows(portion, lineage):
    return jnp.take(portion, lineage, axis=0, mode="clip")


def shards(ensemble, perturbation, ancestors, bathymetry):
    row_count = ensemble.shape[2]
    col_count = ensemble.shape[3]
    total_rows = bathymetry.shape[0]
    first_row = lax.axis_index("slab") * row_count
    widest = 2 * STEPS
    seabed_all = jnp.pad(bathymetry.astype(jnp.float32) * 0.01, ((widest, widest), (0, 0)))
    members = [ensemble[0, 0], ensemble[0, 1], ensemble[0, 2]]
    ocean_floor = lax.dynamic_slice_in_dim(seabed_all, first_row + widest - 2, row_count + 2 * 2, 0)
    global_row = first_row - 2 + jnp.arange(row_count + 2 * 2, dtype=jnp.int32)
    inside = ((global_row >= 0) & (global_row < total_rows))[:, None]
    ocean_floor, inside = (ocean_floor, inside)
    for substep in range(STEPS):
        rims = padded(edge_rows(members, 2), (("slab", 1),), 2)
        widened = attach_rims(members, rims, 2)
        members = list(step_rows(widened[0], widened[1], widened[2], ocean_floor, inside))
    noise = [perturbation[0, 0], perturbation[0, 1], perturbation[0, 2]]
    noise_rims = padded(edge_rows(noise, 1), (("slab", 1),), 1)
    bordered = attach_rims(noise, noise_rims, 1)
    smoothed = jnp.stack(
        [
            (
                4.0 * cell[1:-1]
                + cell[2:]
                + cell[:-2]
                + jnp.roll(cell[1:-1], 1, -1)
                + jnp.roll(cell[1:-1], -1, -1)
            )
            * 0.125
            for cell in bordered
        ]
    )
    lineage = lax.all_gather(ancestors, "ens", axis=0, tiled=True)
    flattened = jnp.stack(members).reshape(1, 3, row_count * col_count)
    pieces = lax.all_to_all(flattened, "ens", split_axis=2, concat_axis=0, tiled=True)
    picked = pick_rows(pieces, lineage)
    returned = lax.all_to_all(picked, "ens", split_axis=0, concat_axis=2, tiled=True)
    selected_parents = returned.reshape(1, 3, row_count, col_count)
    return selected_parents + JITTER * smoothed[None]


def whole_wait(ref, sem):
    pltpu.make_async_copy(ref, ref, sem).wait()


def cycle_kernel(
    n, rows, cols, across,
    ens_ref, pert_ref, anc_ref, bath_ref, out_ref,
    state, noise, sb, seam, seam_sb, bath_v, pieces0, pieces1, pieces2, picked, res, lin_v, lin_s,
    halo_send, halo_recv, lin_send, lin_recv, lin_local, loads,
    a_send, a_recv, b_send, b_recv,
):
    me = lax.axis_index("ens")
    s = lax.axis_index("slab")
    width = cols // across
    pieces = (pieces0, pieces1, pieces2)
    top = STRIP
    bottom = STRIP + rows
    barrier = pltpu.get_barrier_semaphore()

    def peer(t):
        offset = n // 2 + (1 - 2 * (t % 2)) * ((t + 1) // 2)
        return lax.rem(me + offset, n)

    def each_peer(body):
        def run(t, carry):
            body(t, peer(t))
            return carry

        lax.fori_loop(0, n - 1, run, 0)

    def greet(t, to):
        pl.semaphore_signal(barrier, inc=1, device_id={"ens": to}, device_id_type=MESH)

    each_peer(greet)
    pl.semaphore_signal(barrier, inc=1, device_id={"slab": 1 - s}, device_id_type=MESH)

    lin_v[me] = jnp.full((1, LANES), anc_ref[0], jnp.int32)
    inner = pl.multiple_of((1 - s) * (rows - 2 * STRIP), STRIP)
    fills = [
        pltpu.make_async_copy(src, dst, loads.at[i])
        for i, (src, dst) in enumerate(
            (
                (bath_ref, bath_v),
                (ens_ref, state.at[:, pl.ds(top, rows)]),
                (
                    ens_ref.at[:, pl.ds(inner, 2 * STRIP)],
                    seam.at[:, pl.ds(pl.multiple_of(s * STRIP, STRIP), 2 * STRIP)],
                ),
                (pert_ref, noise.at[:, pl.ds(top, rows)]),
            )
        )
    ]
    for fill in fills:
        fill.start()
    zeros = jnp.zeros((STRIP, cols), jnp.float32)
    first = pl.multiple_of(s * rows, STRIP)
    for r in (0, bottom):
        sb[r : r + STRIP] = zeros
        for f in range(3):
            state[f, r : r + STRIP] = zeros
    fills[0].wait()
    for r in range(0, rows, STRIP):
        depth = bath_v[pl.ds(pl.multiple_of(first + r, STRIP), STRIP)]
        sb[top + r : top + r + STRIP] = depth.astype(jnp.float32) * 0.01
    for r in range(0, 3 * STRIP, STRIP):
        depth = bath_v[pl.ds(pl.multiple_of(rows - 2 * STRIP + s * STRIP + r, STRIP), STRIP)]
        seam_sb[r : r + STRIP] = depth.astype(jnp.float32) * 0.01
    fills[1].wait()
    fills[2].wait()

    def east(x):
        return (pltpu.roll(x, cols - 1, 1) - pltpu.roll(x, 1, 1)) * 0.5

    def shifted(ref, r, by):
        if 0 <= r + by <= ref.shape[0] - STRIP:
            return ref[r + by : r + by + STRIP]
        return pltpu.roll(ref[r : r + STRIP], -by % STRIP, 0)

    def heights(cells, floor, r):
        here = slice(r, r + STRIP)
        v = cells.at[2]
        northward = shifted(floor, r, 1) * shifted(v, r, 1) - shifted(floor, r, -1) * shifted(v, r, -1)
        eastward = east(floor[here] * cells[1, here])
        cells[0, here] = cells[0, here] - RATIO * (eastward + northward * 0.5)

    def velocities(cells, r):
        here = slice(r, r + STRIP)
        u = cells[1, here]
        v = cells[2, here]
        h = cells.at[0]
        cells[1, here] = u - RATIO * east(h[here]) + TURNING * v
        northward = (shifted(h, r, 1) - shifted(h, r, -1)) * 0.5
        cells[2, here] = v - RATIO * northward - TURNING * u

    for step in range(STEPS):
        for r in range(top, bottom, STRIP):
            heights(state, sb, r)
        for r in range(top, bottom, STRIP):
            velocities(state, r)

    pl.semaphore_wait(barrier, n)

    edge = pl.multiple_of((1 - s) * (rows - STRIP), STRIP)
    halos = []
    for i, (src, dst, at) in enumerate(
        ((ens_ref, seam, s * 2 * STRIP), (pert_ref, noise, s * (rows + STRIP)))
    ):
        copy = pltpu.make_async_remote_copy(
            src_ref=src.at[:, pl.ds(edge, STRIP)],
            dst_ref=dst.at[:, pl.ds(pl.multiple_of(at, STRIP), STRIP)],
            send_sem=halo_send.at[i],
            recv_sem=halo_recv.at[i],
            device_id={"slab": 1 - s},
            device_id_type=MESH,
        )
        copy.start()
        halos.append(copy)

    def spot(ref, f, index, base):
        r = pl.multiple_of(base + (index // across) * STRIP, STRIP)
        c = pl.multiple_of((index % across) * width, LANES)
        return ref.at[f, pl.ds(r, STRIP), pl.ds(c, width)]

    def deliver(f, to):
        pltpu.make_async_remote_copy(
            src_ref=spot(state, f, to, top),
            dst_ref=pieces[f].at[me],
            send_sem=a_send.at[f],
            recv_sem=a_recv.at[f],
            device_id={"ens": to},
            device_id_type=MESH,
        ).start()

    def keep(f):
        pltpu.make_async_copy(spot(state, f, me, top), pieces[f].at[me], a_recv.at[f]).start()

    def at_seam(to):
        return to // across == (1 - s) * (rows // STRIP - 1)

    def early(t, to):
        @pl.when(jnp.logical_not(at_seam(to)))
        def _():
            deliver(0, to)

    each_peer(early)

    def tell(t, to):
        pltpu.make_async_remote_copy(
            src_ref=lin_v.at[me],
            dst_ref=lin_v.at[me],
            send_sem=lin_send,
            recv_sem=lin_recv,
            device_id={"ens": to},
            device_id_type=MESH,
        ).start()

    each_peer(tell)
    halos[0].wait()
    for step in range(STEPS):
        last = step == STEPS - 1
        for r in range(0, 3 * STRIP, STRIP):
            heights(seam, seam_sb, r)
        for r in range(STRIP, 2 * STRIP, STRIP) if last else range(0, 3 * STRIP, STRIP):
            velocities(seam, r)
    for f in range(3):
        state[f, pl.ds(pl.multiple_of(top + edge, STRIP), STRIP)] = seam[f, STRIP : 2 * STRIP]

    def late(t, to):
        @pl.when(at_seam(to))
        def _():
            deliver(0, to)

    each_peer(late)
    keep(0)
    for f in (1, 2):
        each_peer(lambda t, to, f=f: deliver(f, to))
        keep(f)

    wall = pl.multiple_of(s * (rows + STRIP), STRIP)
    for f in range(3):
        noise[f, pl.ds(wall, STRIP)] = zeros
    fills[3].wait()
    halos[1].wait()
    for f in range(3):
        for r in range(top, bottom, STRIP):
            p = noise[f, r : r + STRIP]
            around = noise[f, r + 1 : r + 1 + STRIP] + noise[f, r - 1 : r - 1 + STRIP]
            total = 4.0 * p + around + pltpu.roll(p, 1, 1) + pltpu.roll(p, cols - 1, 1)
            out_ref[f, r - top : r - top + STRIP] = total * 0.125 * JITTER

    whole_wait(lin_v.at[pl.ds(0, n - 1)], lin_recv)
    fetch = pltpu.make_async_copy(lin_v, lin_s, lin_local)
    fetch.start()
    fetch.wait()

    for f in range(3):
        whole_wait(pieces[f], a_recv.at[f])

        def reply(t, to):
            picked[f, t] = pieces[f][lin_s[to, 0, 0]]
            pltpu.make_async_remote_copy(
                src_ref=picked.at[f, t],
                dst_ref=spot(res, f, me, 0),
                send_sem=b_send.at[f],
                recv_sem=b_recv.at[f],
                device_id={"ens": to},
                device_id_type=MESH,
            ).start()

        each_peer(reply)
        picked[f, n - 1] = pieces[f][lin_s[me, 0, 0]]
        pltpu.make_async_copy(picked.at[f, n - 1], spot(res, f, me, 0), b_recv.at[f]).start()

    for f in range(3):
        whole_wait(res.at[f], b_recv.at[f])
        for r in range(0, rows, STRIP):
            out_ref[f, r : r + STRIP] = res[f, r : r + STRIP] + out_ref[f, r : r + STRIP]
    whole_wait(lin_v.at[pl.ds(0, n - 1)], lin_send)
    for f in range(3):
        whole_wait(pieces[f].at[pl.ds(0, n - 1)], a_send.at[f])
        whole_wait(picked.at[f, pl.ds(0, n - 1)], b_send.at[f])


def cycle(n, ensemble, perturbation, ancestors, bathymetry):
    rows, cols = ensemble.shape[2:]
    across = n * STRIP // rows
    tall = rows + 2 * STRIP
    f32 = jnp.float32
    vmem = pl.BlockSpec(memory_space=pltpu.VMEM)
    hbm = pl.BlockSpec(memory_space=pltpu.HBM)
    dma = pltpu.SemaphoreType.DMA
    held = [
        pltpu.with_memory_space_constraint(x, pltpu.HBM)
        for x in (ensemble[0], perturbation[0], bathymetry)
    ]
    result = pl.pallas_call(
        functools.partial(cycle_kernel, n, rows, cols, across),
        out_shape=jax.ShapeDtypeStruct((3, rows, cols), f32),
        in_specs=[hbm, hbm, pl.BlockSpec(memory_space=pltpu.SMEM), hbm],
        out_specs=vmem,
        scratch_shapes=[
            pltpu.VMEM((3, tall, cols), f32),
            pltpu.VMEM((3, tall, cols), f32),
            pltpu.VMEM((tall, cols), f32),
            pltpu.VMEM((3, 3 * STRIP, cols), f32),
            pltpu.VMEM((3 * STRIP, cols), f32),
            pltpu.VMEM(bathymetry.shape, jnp.int32),
            pltpu.VMEM((n, STRIP, cols // across), f32),
            pltpu.VMEM((n, STRIP, cols // across), f32),
            pltpu.VMEM((n, STRIP, cols // across), f32),
            pltpu.VMEM((3, n, STRIP, cols // across), f32),
            pltpu.VMEM((3, rows, cols), f32),
            pltpu.VMEM((n, 1, LANES), jnp.int32),
            pltpu.SMEM((n, 1, LANES), jnp.int32),
            dma((2,)), dma((2,)), dma(()), dma(()), dma(()), dma((4,)),
            dma((3,)), dma((3,)), dma((3,)), dma((3,)),
        ],
        compiler_params=pltpu.CompilerParams(collective_id=0, has_side_effects=True, vmem_limit_bytes=24 << 20),
        name="cycle",
    )(*held[:2], ancestors, held[2])
    return result[None]


def fits(mesh, ensemble):
    n, slabs = mesh.shape["ens"], mesh.shape["slab"]
    rows, cols = ensemble.shape[2] // slabs, ensemble.shape[3]
    strips = rows // STRIP
    if slabs != 2 or ensemble.shape[0] != n or rows % STRIP or n % strips:
        return False
    across = n // strips
    return cols % (across * LANES) == 0


def solution(mesh):
    in_specs = (P("ens", None, "slab", None), P("ens", None, "slab", None), P("ens"), P())
    out_specs = P("ens", None, "slab", None)

    def run(ensemble, perturbation, ancestors, bathymetry):
        body = functools.partial(cycle, mesh.shape["ens"]) if fits(mesh, ensemble) else shards
        mapped = jax.shard_map(body, mesh=mesh, in_specs=in_specs, out_specs=out_specs, check_vma=False)
        return mapped(ensemble, perturbation, ancestors, bathymetry)

    return run
```
